32 devices in a mesh: pb: 8 (over y, x, core), ka: 4 (over z).
Axes of the slice: x: 2, y: 2, z: 4, core: 2. Of those that a mesh axis runs over, the one named last changes fastest.
Arguments:
- coupling: bfloat16 [2, 320, 4800, 320], P(None, 'ka', 'pb'), may hold values from -0.019897461 to 0.019897461
- kpoints: int32 [3, 16], replicated, may hold values from 0 to 99
- qpoints: int32 [3, 32], replicated, may hold values from 0 to 99
- electron_cells: int32 [3, 320], replicated, may hold values from -6 to 6
- phonon_cells: int32 [3, 320], replicated, may hold values from -6 to 6
- phonon_modes: bfloat16 [32, 2, 120, 120], P('pb'), may hold values from -0.375 to 0.375
- band_vectors: bfloat16 [32, 16, 2, 40, 40], P('pb', 'ka'), may hold values from -0.625 to 0.625
- energies_kq: float32 [32, 16, 40], P('pb', 'ka'), may hold values from -0.5 to 0.5
- occupations_kq: float32 [32, 16, 40], P('pb', 'ka'), may hold values from 0 to 1
- energy_k: float32 [16], P('ka'), may hold values from -0.5 to 0.5
- occupation_k: float32 [16], P('ka'), may hold values from 0 to 1
- frequencies: float32 [32, 120], P('pb'), may hold values from 0.02 to 0.2
- bose_factors: float32 [32, 120], P('pb'), may hold values from 0.1 to 5
Outputs:
- electron_width: float32 [16, 120], P('ka')
- phonon_width: float32 [32, 120], P('pb')
The draws below stay inside these ranges and needn't reach their ends.
All inputs are finite; a program needn't handle non-finite values.
Results may differ from the reference program's by a relative error of at most 0.0066.
Values may be sent and summed in bfloat16 or wider, within the bound.
A program may use at most 320 MiB of HBM per device.

```python
import math
import jax
import jax.numpy as jnp
from jax import lax

NB = 40
MODES = 120
CE = 320
CP = 320
NG = 100
QD = 4
PAIRS = 4800
KTOT = 16
QTOT = 32


def set_ends(result, key, least, top_value):
    place = [jax.random.randint(jax.random.fold_in(key, axis), (), 0, length) for axis, length in enumerate(result.shape)]
    main_axis = result.shape.index(max(result.shape))
    beside = place[:main_axis] + [(place[main_axis] + 1) % result.shape[main_axis]] + place[main_axis + 1:]
    return result.at[tuple(place)].set(least).at[tuple(beside)].set(top_value)


def level_of(key, extent, shards, smallest, high):
    gain = 1.0
    for position, shards_of in shards:
        steps = jax.random.uniform(jax.random.fold_in(jax.random.fold_in(key, 6), position), (shards_of,), jnp.float32, smallest / len(shards), high / len(shards))
        gain = gain * jnp.repeat(jnp.exp(steps), extent[position] // shards_of).reshape((-1,) + (1,) * (len(extent) - 1 - position))
    return gain


def centred(own_key, dims, scale, limit, split=(), held_as=jnp.bfloat16):
    array = scale * jax.random.normal(own_key, dims, jnp.float32)
    if split:
        array = array * level_of(own_key, dims, split, -0.22, 0.18)
    return jnp.clip(array, -limit, limit).astype(held_as)


def setup_inputs(seed: int = 0) -> dict:
    seeds = jax.random.split(jax.random.key(seed), 14)
    coupling = centred(seeds[0], (2, CE, PAIRS, CP), 0.003125, 0.019897461, ((1, 4), (2, 8)))
    kpoints = set_ends(jax.random.randint(seeds[1], (3, KTOT), 0, NG), jax.random.fold_in(seeds[1], 1), 0, NG - 1).astype(jnp.int32)
    qpoints = set_ends(jax.random.randint(seeds[2], (3, QTOT), 0, NG), jax.random.fold_in(seeds[2], 1), 0, NG - 1).astype(jnp.int32)
    electron_cells = set_ends(jax.random.randint(seeds[3], (3, CE), -6, 7), jax.random.fold_in(seeds[3], 1), -6, 6).astype(jnp.int32)
    phonon_cells = set_ends(jax.random.randint(seeds[4], (3, CP), -6, 7), jax.random.fold_in(seeds[4], 1), -6, 6).astype(jnp.int32)
    phonon_modes = centred(seeds[5], (QTOT, 2, MODES, MODES), (2 * MODES) ** -0.5, 0.375, ((0, 8),))
    band_vectors = centred(seeds[6], (QTOT, KTOT, 2, NB, NB), (2 * NB) ** -0.5, 0.625, ((0, 8), (1, 4)))
    energies_kq = jnp.clip(jax.random.uniform(seeds[7], (QTOT, KTOT, NB), jnp.float32, -0.5, 0.5) * level_of(seeds[7], (QTOT, KTOT, NB), ((0, 8), (1, 4)), -0.4, 0.0), -0.5, 0.5)
    occupations_kq = jnp.clip(1.0 * jax.random.uniform(seeds[8], (QTOT, KTOT, NB), jnp.float32) ** level_of(seeds[8], (QTOT, KTOT, NB), ((0, 8), (1, 4)), -0.2, 0.2), 0.0, 1.0)
    energy_k = jnp.clip(jax.random.uniform(seeds[9], (KTOT,), jnp.float32, -0.5, 0.5) * level_of(seeds[9], (KTOT,), ((0, 4),), -0.4, 0.0), -0.5, 0.5)
    occupation_k = jnp.clip(1.0 * jax.random.uniform(seeds[10], (KTOT,), jnp.float32) ** level_of(seeds[10], (KTOT,), ((0, 4),), -0.2, 0.2), 0.0, 1.0)
    frequencies = jnp.clip(jnp.exp(math.log(0.2) - 2.3025851 * jax.random.uniform(seeds[11], (QTOT, MODES), jnp.float32) ** level_of(seeds[11], (QTOT, MODES), ((0, 8),), -0.2, 0.2)), 0.02, 0.2)
    bose_factors = jnp.clip(jnp.exp(math.log(5.0) - 3.912023 * jax.random.uniform(seeds[12], (QTOT, MODES), jnp.float32) ** level_of(seeds[12], (QTOT, MODES), ((0, 8),), -0.2, 0.2)), 0.1, 5.0)
    return {"coupling": coupling, "kpoints": kpoints, "qpoints": qpoints, "electron_cells": electron_cells, "phonon_cells": phonon_cells, "phonon_modes": phonon_modes, "band_vectors": band_vectors, "energies_kq": energies_kq, "occupations_kq": occupations_kq, "energy_k": energy_k, "occupation_k": occupation_k, "frequencies": frequencies, "bose_factors": bose_factors}


smearing = 0.05

def phase_table(points, cells):
    product = points[0][:, None] * cells[0][None, :] + points[1][:, None] * cells[1][None, :] + points[2][:, None] * cells[2][None, :]
    angle = jnp.mod(product, NG).astype(jnp.float32) * (2.0 * math.pi / NG)
    return (jnp.cos(angle).astype(jnp.bfloat16), jnp.sin(angle).astype(jnp.bfloat16))

def gaussian(offset):
    return jnp.exp(-0.5 * (offset / smearing) ** 2) / (smearing * math.sqrt(2.0 * math.pi))

def contract_last(left, right):
    return lax.dot_general(left, right, (((1,), (1,)), ((), ())), preferred_element_type=jnp.float32)

def floated(form, left, right):
    return jnp.einsum(form, left.astype(jnp.float32), right.astype(jnp.float32))

def widths(bloch_real, bloch_imag, modes, vectors, levels, filled, energy_k, occupation_k, omega, bose):
    mode_real = modes[:, 0]
    mode_imag = modes[:, 1]
    moded_real = (floated('kqnm,qmv->kqnv', bloch_real, mode_real) - floated('kqnm,qmv->kqnv', bloch_imag, mode_imag)).astype(jnp.bfloat16)
    moded_imag = (floated('kqnm,qmv->kqnv', bloch_real, mode_imag) + floated('kqnm,qmv->kqnv', bloch_imag, mode_real)).astype(jnp.bfloat16)
    vector_real = vectors[:, :, 0]
    vector_imag = vectors[:, :, 1]
    band_real = floated('qknb,kqnv->kqbv', vector_real, moded_real) + floated('qknb,kqnv->kqbv', vector_imag, moded_imag)
    band_imag = floated('qknb,kqnv->kqbv', vector_real, moded_imag) - floated('qknb,kqnv->kqbv', vector_imag, moded_real)
    weight = band_real * band_real + band_imag * band_imag
    level_kq = jnp.transpose(levels, (1, 0, 2))[..., None]
    filled_kq = jnp.transpose(filled, (1, 0, 2))[..., None]
    offset = energy_k[:, None, None, None] - level_kq
    freq = omega[None, :, None, :]
    boson = bose[None, :, None, :]
    absorb = gaussian(offset + freq)
    emit = gaussian(offset - freq)
    electron = lax.optimization_barrier(jnp.sum(weight * ((boson + filled_kq) * absorb + (boson + 1.0 - filled_kq) * emit), axis=(1, 2)))
    phonon = lax.optimization_barrier(jnp.sum(weight * (occupation_k[:, None, None, None] - filled_kq) * absorb, axis=(0, 2)))
    return (electron, phonon)

def reference(coupling, kpoints, qpoints, electron_cells, phonon_cells, phonon_modes, band_vectors, energies_kq, occupations_kq, energy_k, occupation_k, frequencies, bose_factors):
    cos_k, sin_k = phase_table(kpoints, electron_cells)
    cos_q, sin_q = phase_table(qpoints, phonon_cells)
    real_flat = coupling[0].reshape(CE * PAIRS, CP)
    imag_flat = coupling[1].reshape(CE * PAIRS, CP)
    count = QTOT // QD

    def block_step(total, index):
        start = (index * QD).astype(jnp.int32)
        cos_block = lax.dynamic_slice_in_dim(cos_q, start, QD, 0)
        sin_block = lax.dynamic_slice_in_dim(sin_q, start, QD, 0)
        half_real = (contract_last(cos_block, real_flat) - contract_last(sin_block, imag_flat)).astype(jnp.bfloat16).reshape(QD, CE, PAIRS)
        half_imag = (contract_last(cos_block, imag_flat) + contract_last(sin_block, real_flat)).astype(jnp.bfloat16).reshape(QD, CE, PAIRS)
        bloch_real = (floated('kr,qrp->kqp', cos_k, half_real) - floated('kr,qrp->kqp', sin_k, half_imag)).astype(jnp.bfloat16)
        bloch_imag = (floated('kr,qrp->kqp', cos_k, half_imag) + floated('kr,qrp->kqp', sin_k, half_real)).astype(jnp.bfloat16)
        bloch_real = bloch_real.reshape(KTOT, QD, NB, MODES)
        bloch_imag = bloch_imag.reshape(KTOT, QD, NB, MODES)
        electron, phonon = widths(bloch_real, bloch_imag, lax.dynamic_slice_in_dim(phonon_modes, start, QD, 0), lax.dynamic_slice_in_dim(band_vectors, start, QD, 0), lax.dynamic_slice_in_dim(energies_kq, start, QD, 0), lax.dynamic_slice_in_dim(occupations_kq, start, QD, 0), energy_k, occupation_k, lax.dynamic_slice_in_dim(frequencies, start, QD, 0), lax.dynamic_slice_in_dim(bose_factors, start, QD, 0))
        return (total + electron / (QTOT * NB), phonon / (KTOT * NB))
    initial = jnp.zeros((KTOT, MODES), jnp.float32)
    electron_width, phonon_blocks = lax.scan(block_step, initial, jnp.arange(count, dtype=jnp.int32))
    return (electron_width, phonon_blocks.reshape(QTOT, MODES))
```

```python
import functools
import math

import jax
import jax.numpy as jnp
from jax import lax
from jax.experimental import pallas as pl
from jax.experimental.pallas import tpu as pltpu
from jax.sharding import PartitionSpec as P

NB = 40
MODES = 120
NG = 100


smearing = 0.05


def phase_table(points, cells):
    product = (
        points[0][:, None] * cells[0][None, :]
        + points[1][:, None] * cells[1][None, :]
        + points[2][:, None] * cells[2][None, :]
    )
    angle = jnp.mod(product, NG).astype(jnp.float32) * (2.0 * math.pi / NG)
    return (jnp.cos(angle).astype(jnp.bfloat16), jnp.sin(angle).astype(jnp.bfloat16))


def gaussian(offset):
    return jnp.exp(-0.5 * (offset / smearing) ** 2) / (smearing * math.sqrt(2.0 * math.pi))


def contract_last(left, right):
    return lax.dot_general(
        left, right, (((1,), (1,)), ((), ())), preferred_element_type=jnp.float32
    )


def mixed(form, left, right):
    return jnp.einsum(form, left, right, preferred_element_type=jnp.float32)


def widths(
    bloch_real, bloch_imag, modes, vectors, levels, filled, energy_k, occupation_k, omega, bose
):
    mode_real = modes[:, 0]
    mode_imag = modes[:, 1]
    moded_real = (
        mixed("kqnm,qmv->kqnv", bloch_real, mode_real)
        - mixed("kqnm,qmv->kqnv", bloch_imag, mode_imag)
    ).astype(jnp.bfloat16)
    moded_imag = (
        mixed("kqnm,qmv->kqnv", bloch_real, mode_imag)
        + mixed("kqnm,qmv->kqnv", bloch_imag, mode_real)
    ).astype(jnp.bfloat16)
    vector_real = vectors[:, :, 0]
    vector_imag = vectors[:, :, 1]
    band_real = mixed("qknb,kqnv->kqbv", vector_real, moded_real) + mixed(
        "qknb,kqnv->kqbv", vector_imag, moded_imag
    )
    band_imag = mixed("qknb,kqnv->kqbv", vector_real, moded_imag) - mixed(
        "qknb,kqnv->kqbv", vector_imag, moded_real
    )
    weight = band_real * band_real + band_imag * band_imag
    level_kq = jnp.transpose(levels, (1, 0, 2))[..., None]
    filled_kq = jnp.transpose(filled, (1, 0, 2))[..., None]
    offset = energy_k[:, None, None, None] - level_kq
    freq = omega[None, :, None, :]
    boson = bose[None, :, None, :]
    absorb = gaussian(offset + freq)
    emit = gaussian(offset - freq)
    electron = jnp.sum(
        weight * ((boson + filled_kq) * absorb + (boson + 1.0 - filled_kq) * emit), axis=(1, 2)
    )
    phonon = jnp.sum(weight * (occupation_k[:, None, None, None] - filled_kq) * absorb, axis=(0, 2))
    return (electron, phonon)


MESH = pl.DeviceIdType.MESH
LANES = 128


def bloch_kernel(
    cells_block, tile, last, wq_ref, wk_ref, x_ref, out_ref,
    half, parts, recv, send_sem, recv_sem,
):
    pairs_step = pl.program_id(0)
    cell_step = pl.program_id(1)
    tiles = pl.num_programs(0)
    cell_steps = pl.num_programs(1)
    bands, kas = lax.axis_size("pb"), lax.axis_size("ka")
    devices = bands * kas
    me = lax.axis_index("pb") * kas + lax.axis_index("ka")
    columns = wq_ref.shape[0]
    cells = half.shape[1] // columns
    groups = parts.shape[2]
    mine = groups // bands
    rows = parts.shape[3] // 2
    barrier = pltpu.get_barrier_semaphore()

    @pl.when((pairs_step == 0) & (cell_step == 0))
    def _():
        def greet(step, carry):
            peer = lax.rem(me + step, devices)
            pl.semaphore_signal(
                barrier, inc=1, device_id={"pb": peer // kas, "ka": lax.rem(peer, kas)},
                device_id_type=MESH,
            )
            return carry

        lax.fori_loop(1, devices, greet, 0)

    for cell in range(cells_block):
        right = jnp.concatenate([x_ref[0, cell], x_ref[1, cell]], axis=0)
        product = jnp.dot(wq_ref[...], right, preferred_element_type=jnp.float32)
        row = cell_step * cells_block + cell
        for lane in range(tile // LANES):
            half[lane, pl.ds(row, columns, stride=cells), :] = product[
                :, lane * LANES : (lane + 1) * LANES
            ]

    def strip(index):
        start = pl.multiple_of(index * cells, cells)
        return jnp.concatenate(
            [half[lane, pl.ds(start, cells), :] for lane in range(tile // LANES)], axis=1
        ).astype(jnp.bfloat16)

    @pl.when(cell_step == cell_steps - 1)
    def _():
        def contract(group, carry):
            sums = []
            for member in range(2):
                q = group * 2 + member
                right = jnp.concatenate([strip(q), strip(columns // 2 + q)], axis=0)
                sums.append(
                    jnp.dot(wk_ref[...], right, preferred_element_type=jnp.float32)
                )
            for ka in range(kas):
                block = slice(ka * rows, (ka + 1) * rows)
                parts[pairs_step, ka, group] = jnp.concatenate(
                    [sums[0][block], sums[1][block]], axis=0
                ).astype(jnp.bfloat16)
            return carry

        lax.fori_loop(0, groups, contract, 0, unroll=4)

    @pl.when((cell_step == cell_steps - 1) & (pairs_step == 0))
    def _():
        pl.semaphore_wait(barrier, devices - 1)

    def send(index, width):
        def one(step, carry):
            peer = lax.rem(me + step, devices)
            to_pb, to_ka = peer // kas, lax.rem(peer, kas)
            pltpu.make_async_remote_copy(
                src_ref=parts.at[index, to_ka, pl.ds(to_pb * mine, mine), :, pl.ds(0, width)],
                dst_ref=recv.at[index, me, :, :, pl.ds(0, width)],
                send_sem=send_sem.at[index],
                recv_sem=recv_sem.at[index],
                device_id={"pb": to_pb, "ka": to_ka},
                device_id_type=MESH,
            ).start()
            return carry

        lax.fori_loop(1, devices, one, 0)

    @pl.when((cell_step == cell_steps - 1) & (pairs_step < tiles - 1))
    def _():
        send(pairs_step, tile)

    @pl.when((cell_step == cell_steps - 1) & (pairs_step == tiles - 1))
    def _():
        count = recv.shape[0]
        send(count - 1, last)
        my_pb, my_ka = lax.axis_index("pb"), lax.axis_index("ka")
        for index in range(count):
            recv[index, me] = parts[index, my_ka, pl.ds(my_pb * mine, mine)]
        for index in range(count):
            width = tile if index < count - 1 else last
            window = recv.at[index, pl.ds(1, devices - 1), :, :, pl.ds(0, width)]
            pltpu.make_async_copy(window, window, send_sem.at[index]).wait()
            pltpu.make_async_copy(window, window, recv_sem.at[index]).wait()
            for band in range(bands):
                total = recv[index, band * kas, :, :, :width].astype(jnp.float32)
                for ka in range(1, kas):
                    total = total + recv[index, band * kas + ka, :, :, :width].astype(jnp.float32)
                out_ref[band, :, :, index * tile : index * tile + width] = total.astype(
                    jnp.bfloat16
                )


def bloch(coupling, wq, wk, q_local, k_local):
    bands, kas = lax.axis_size("pb"), lax.axis_size("ka")
    devices = bands * kas
    parts_count, cells, pairs, phonons = coupling.shape
    moved = jnp.transpose(coupling, (0, 1, 3, 2))
    padded = -(-pairs // LANES) * LANES
    if pairs < LANES:
        moved = jnp.pad(moved, ((0, 0), (0, 0), (0, 0), (0, LANES - pairs)))
    tile = min(2 * LANES, padded)
    tiles = -(-padded // tile)
    last = padded - (tiles - 1) * tile
    cells_block = 16
    columns = wq.shape[0]
    groups = columns // 4
    mine = q_local // 2
    rows = 4 * k_local
    result = pl.pallas_call(
        functools.partial(bloch_kernel, cells_block, tile, last),
        grid=(tiles, cells // cells_block),
        in_specs=[
            pl.BlockSpec(wq.shape, lambda t, e: (0, 0)),
            pl.BlockSpec(wk.shape, lambda t, e: (0, 0)),
            pl.BlockSpec((parts_count, cells_block, phonons, tile), lambda t, e: (0, e, 0, t)),
        ],
        out_specs=pl.BlockSpec((bands, mine, rows, padded), lambda t, e: (0, 0, 0, 0)),
        out_shape=jax.ShapeDtypeStruct((bands, mine, rows, padded), jnp.bfloat16),
        scratch_shapes=[
            pltpu.VMEM((tile // LANES, columns * cells, LANES), jnp.float32),
            pltpu.VMEM((tiles, kas, groups, rows, tile), jnp.bfloat16),
            pltpu.VMEM((tiles, devices, mine, rows, tile), jnp.bfloat16),
            pltpu.SemaphoreType.DMA((tiles,)),
            pltpu.SemaphoreType.DMA((tiles,)),
        ],
        compiler_params=pltpu.CompilerParams(
            collective_id=0,
            has_side_effects=True,
            dimension_semantics=("arbitrary", "arbitrary"),
            vmem_limit_bytes=60 * 1024 * 1024,
        ),
        name="bloch",
    )(wq, wk, moved)
    return result[..., :pairs]


def sums_kernel(electron_ref, phonon_ref, electron_out, phonon_out, got_e, got_p, send, recv_e, recv_p):
    bands, kas = lax.axis_size("pb"), lax.axis_size("ka")
    my_pb, my_ka = lax.axis_index("pb"), lax.axis_index("ka")
    barrier = pltpu.get_barrier_semaphore()
    for step in range(1, bands):
        pl.semaphore_signal(
            barrier, inc=1, device_id={"pb": lax.rem(my_pb + step, bands), "ka": my_ka},
            device_id_type=MESH,
        )
    for step in range(1, kas):
        pl.semaphore_signal(
            barrier, inc=1, device_id={"pb": my_pb, "ka": lax.rem(my_ka + step, kas)},
            device_id_type=MESH,
        )
    pl.semaphore_wait(barrier, bands + kas - 2)
    copies = []
    for step in range(1, bands):
        copies.append(pltpu.make_async_remote_copy(
            electron_ref, got_e.at[my_pb], send.at[step - 1], recv_e.at[step - 1],
            device_id={"pb": lax.rem(my_pb + step, bands), "ka": my_ka}, device_id_type=MESH,
        ))
    for step in range(1, kas):
        copies.append(pltpu.make_async_remote_copy(
            phonon_ref, got_p.at[my_ka], send.at[bands + step - 2], recv_p.at[step - 1],
            device_id={"pb": my_pb, "ka": lax.rem(my_ka + step, kas)}, device_id_type=MESH,
        ))
    for copy in copies:
        copy.start()
    got_e[my_pb] = electron_ref[...]
    got_p[my_ka] = phonon_ref[...]
    for copy in copies:
        copy.wait()
    total = got_e[0]
    for step in range(1, bands):
        total = total + got_e[step]
    electron_out[...] = total
    total = got_p[0]
    for step in range(1, kas):
        total = total + got_p[step]
    phonon_out[...] = total


def exchange(electron, phonon):
    bands, kas = lax.axis_size("pb"), lax.axis_size("ka")
    whole = pl.BlockSpec(memory_space=pltpu.VMEM)
    return pl.pallas_call(
        sums_kernel,
        in_specs=[whole, whole],
        out_specs=[whole, whole],
        out_shape=[
            jax.ShapeDtypeStruct(electron.shape, electron.dtype),
            jax.ShapeDtypeStruct(phonon.shape, phonon.dtype),
        ],
        scratch_shapes=[
            pltpu.VMEM((bands, *electron.shape), jnp.float32),
            pltpu.VMEM((kas, *phonon.shape), jnp.float32),
            pltpu.SemaphoreType.DMA((bands + kas - 2,)),
            pltpu.SemaphoreType.DMA((bands - 1,)),
            pltpu.SemaphoreType.DMA((kas - 1,)),
        ],
        compiler_params=pltpu.CompilerParams(collective_id=1, has_side_effects=True),
        name="sums",
    )(electron, phonon)


def on_device(
    coupling,
    kpoints,
    qpoints,
    electron_cells,
    phonon_cells,
    phonon_modes,
    band_vectors,
    energies_kq,
    occupations_kq,
    energy_k,
    occupation_k,
    frequencies,
    bose_factors,
):
    k_local = energy_k.shape[0]
    q_local = frequencies.shape[0]
    cells_local = coupling.shape[1]
    bands, kas = lax.axis_size("pb"), lax.axis_size("ka")
    q_total = q_local * bands
    k_total = k_local * kas
    cos_q, sin_q = phase_table(qpoints, phonon_cells)
    own_cells = lax.dynamic_slice_in_dim(
        electron_cells, lax.axis_index("ka") * cells_local, cells_local, 1
    )
    cos_k, sin_k = phase_table(kpoints, own_cells)
    wq = jnp.concatenate(
        [jnp.concatenate([cos_q, -sin_q], 1), jnp.concatenate([sin_q, cos_q], 1)], 0
    )
    wk = jnp.stack(
        [jnp.concatenate([cos_k, -sin_k], 1), jnp.concatenate([sin_k, cos_k], 1)], 1
    ).reshape(2 * k_total, 2 * cells_local)
    values = bloch(coupling, wq, wk, q_local, k_local)
    values = values.reshape(bands, q_local // 2, 2, k_local, 2, -1)
    values = jnp.transpose(values, (4, 3, 1, 2, 0, 5)).reshape(2, k_local, q_local, NB, MODES)
    electron, phonon = widths(
        values[0],
        values[1],
        phonon_modes,
        band_vectors,
        energies_kq,
        occupations_kq,
        energy_k,
        occupation_k,
        frequencies,
        bose_factors,
    )
    electron_width, phonon_width = exchange(electron / (q_total * NB), phonon / (k_total * NB))
    return (electron_width, phonon_width)


def solution(mesh):
    in_specs = (
        P(None, "ka", "pb", None),
        P(),
        P(),
        P(),
        P(),
        P("pb", None, None, None),
        P("pb", "ka", None, None, None),
        P("pb", "ka", None),
        P("pb", "ka", None),
        P("ka"),
        P("ka"),
        P("pb", None),
        P("pb", None),
    )
    out_specs = (P("ka", None), P("pb", None))
    return jax.shard_map(
        on_device, mesh=mesh, in_specs=in_specs, out_specs=out_specs, check_vma=False
    )
```

```python
import functools
import math

import jax
import jax.numpy as jnp
from jax import lax
from jax.experimental import pallas as pl
from jax.experimental.pallas import tpu as pltpu
from jax.sharding import PartitionSpec as P

NB = 40
MODES = 120
NG = 100


smearing = 0.05


def phase_table(points, cells):
    product = (
        points[0][:, None] * cells[0][None, :]
        + points[1][:, None] * cells[1][None, :]
        + points[2][:, None] * cells[2][None, :]
    )
    angle = jnp.mod(product, NG).astype(jnp.float32) * (2.0 * math.pi / NG)
    return (jnp.cos(angle).astype(jnp.bfloat16), jnp.sin(angle).astype(jnp.bfloat16))


def gaussian(offset):
    return jnp.exp(-0.5 * (offset / smearing) ** 2) / (smearing * math.sqrt(2.0 * math.pi))


def contract_last(left, right):
    return lax.dot_general(
        left, right, (((1,), (1,)), ((), ())), preferred_element_type=jnp.float32
    )


def mixed(form, left, right):
    return jnp.einsum(form, left, right, preferred_element_type=jnp.float32)


def widths(
    bloch_real, bloch_imag, modes, vectors, levels, filled, energy_k, occupation_k, omega, bose
):
    mode_real = modes[:, 0]
    mode_imag = modes[:, 1]
    moded_real = (
        mixed("kqnm,qmv->kqnv", bloch_real, mode_real)
        - mixed("kqnm,qmv->kqnv", bloch_imag, mode_imag)
    ).astype(jnp.bfloat16)
    moded_imag = (
        mixed("kqnm,qmv->kqnv", bloch_real, mode_imag)
        + mixed("kqnm,qmv->kqnv", bloch_imag, mode_real)
    ).astype(jnp.bfloat16)
    vector_real = vectors[:, :, 0]
    vector_imag = vectors[:, :, 1]
    band_real = mixed("qknb,kqnv->kqbv", vector_real, moded_real) + mixed(
        "qknb,kqnv->kqbv", vector_imag, moded_imag
    )
    band_imag = mixed("qknb,kqnv->kqbv", vector_real, moded_imag) - mixed(
        "qknb,kqnv->kqbv", vector_imag, moded_real
    )
    weight = band_real * band_real + band_imag * band_imag
    level_kq = jnp.transpose(levels, (1, 0, 2))[..., None]
    filled_kq = jnp.transpose(filled, (1, 0, 2))[..., None]
    offset = energy_k[:, None, None, None] - level_kq
    freq = omega[None, :, None, :]
    boson = bose[None, :, None, :]
    absorb = gaussian(offset + freq)
    emit = gaussian(offset - freq)
    electron = jnp.sum(
        weight * ((boson + filled_kq) * absorb + (boson + 1.0 - filled_kq) * emit), axis=(1, 2)
    )
    phonon = jnp.sum(weight * (occupation_k[:, None, None, None] - filled_kq) * absorb, axis=(0, 2))
    return (electron, phonon)


MESH = pl.DeviceIdType.MESH
LANES = 128


def bloch_kernel(
    cells_block, tile, last, wq_ref, wk_ref, x_ref, out_ref,
    half, parts, recv, send_sem, recv_sem,
):
    pairs_step = pl.program_id(0)
    cell_step = pl.program_id(1)
    tiles = pl.num_programs(0)
    cell_steps = pl.num_programs(1)
    bands, kas = lax.axis_size("pb"), lax.axis_size("ka")
    devices = bands * kas
    me = lax.axis_index("pb") * kas + lax.axis_index("ka")
    columns = wq_ref.shape[0]
    cells = half.shape[1] // columns
    groups = parts.shape[2]
    mine = groups // bands
    rows = parts.shape[3] // 2
    barrier = pltpu.get_barrier_semaphore()

    @pl.when((pairs_step == 0) & (cell_step == 0))
    def _():
        def greet(step, carry):
            peer = lax.rem(me + step, devices)
            pl.semaphore_signal(
                barrier, inc=1, device_id={"pb": peer // kas, "ka": lax.rem(peer, kas)},
                device_id_type=MESH,
            )
            return carry

        lax.fori_loop(1, devices, greet, 0)

    for cell in range(cells_block):
        right = jnp.concatenate([x_ref[0, cell], x_ref[1, cell]], axis=0)
        product = jnp.dot(wq_ref[...], right, preferred_element_type=jnp.float32)
        row = cell_step * cells_block + cell
        for lane in range(tile // LANES):
            half[lane, pl.ds(row, columns, stride=cells), :] = product[
                :, lane * LANES : (lane + 1) * LANES
            ]

    def strip(index):
        start = pl.multiple_of(index * cells, cells)
        return jnp.concatenate(
            [half[lane, pl.ds(start, cells), :] for lane in range(tile // LANES)], axis=1
        ).astype(jnp.bfloat16)

    @pl.when(cell_step == cell_steps - 1)
    def _():
        def contract(group, carry):
            sums = []
            for member in range(2):
                q = group * 2 + member
                right = jnp.concatenate([strip(q), strip(columns // 2 + q)], axis=0)
                sums.append(
                    jnp.dot(wk_ref[...], right, preferred_element_type=jnp.float32)
                )
            for ka in range(kas):
                block = slice(ka * rows, (ka + 1) * rows)
                parts[pairs_step, ka, group] = jnp.concatenate(
                    [sums[0][block], sums[1][block]], axis=0
                ).astype(jnp.bfloat16)
            return carry

        lax.fori_loop(0, groups, contract, 0, unroll=4)

    @pl.when((cell_step == cell_steps - 1) & (pairs_step == 0))
    def _():
        pl.semaphore_wait(barrier, devices - 1)

    def send(index, width):
        def one(step, carry):
            peer = lax.rem(me + step, devices)
            to_pb, to_ka = peer // kas, lax.rem(peer, kas)
            pltpu.make_async_remote_copy(
                src_ref=parts.at[index, to_ka, pl.ds(to_pb * mine, mine), :, pl.ds(0, width)],
                dst_ref=recv.at[index, me, :, :, pl.ds(0, width)],
                send_sem=send_sem.at[index],
                recv_sem=recv_sem.at[index],
                device_id={"pb": to_pb, "ka": to_ka},
                device_id_type=MESH,
            ).start()
            return carry

        lax.fori_loop(1, devices, one, 0)

    @pl.when((cell_step == cell_steps - 1) & (pairs_step < tiles - 1))
    def _():
        send(pairs_step, tile)

    @pl.when((cell_step == cell_steps - 1) & (pairs_step == tiles - 1))
    def _():
        count = recv.shape[0]
        send(count - 1, last)
        my_pb, my_ka = lax.axis_index("pb"), lax.axis_index("ka")
        for index in range(count):
            recv[index, me] = parts[index, my_ka, pl.ds(my_pb * mine, mine)]
        for index in range(count):
            width = tile if index < count - 1 else last
            window = recv.at[index, pl.ds(1, devices - 1), :, :, pl.ds(0, width)]
            pltpu.make_async_copy(window, window, send_sem.at[index]).wait()
            pltpu.make_async_copy(window, window, recv_sem.at[index]).wait()
            for band in range(bands):
                total = recv[index, band * kas, :, :, :width].astype(jnp.float32)
                for ka in range(1, kas):
                    total = total + recv[index, band * kas + ka, :, :, :width].astype(jnp.float32)
                out_ref[band, :, :, index * tile : index * tile + width] = total.astype(
                    jnp.bfloat16
                )


def bloch(coupling, wq, wk, q_local, k_local):
    bands, kas = lax.axis_size("pb"), lax.axis_size("ka")
    devices = bands * kas
    parts_count, cells, pairs, phonons = coupling.shape
    moved = jnp.transpose(coupling, (0, 1, 3, 2))
    padded = -(-pairs // LANES) * LANES
    if pairs < LANES:
        moved = jnp.pad(moved, ((0, 0), (0, 0), (0, 0), (0, LANES - pairs)))
    tile = min(2 * LANES, padded)
    tiles = -(-padded // tile)
    last = padded - (tiles - 1) * tile
    cells_block = 16
    columns = wq.shape[0]
    groups = columns // 4
    mine = q_local // 2
    rows = 4 * k_local
    result = pl.pallas_call(
        functools.partial(bloch_kernel, cells_block, tile, last),
        grid=(tiles, cells // cells_block),
        in_specs=[
            pl.BlockSpec(wq.shape, lambda t, e: (0, 0)),
            pl.BlockSpec(wk.shape, lambda t, e: (0, 0)),
            pl.BlockSpec((parts_count, cells_block, phonons, tile), lambda t, e: (0, e, 0, t)),
        ],
        out_specs=pl.BlockSpec((bands, mine, rows, padded), lambda t, e: (0, 0, 0, 0)),
        out_shape=jax.ShapeDtypeStruct((bands, mine, rows, padded), jnp.bfloat16),
        scratch_shapes=[
            pltpu.VMEM((tile // LANES, columns * cells, LANES), jnp.float32),
            pltpu.VMEM((tiles, kas, groups, rows, tile), jnp.bfloat16),
            pltpu.VMEM((tiles, devices, mine, rows, tile), jnp.bfloat16),
            pltpu.SemaphoreType.DMA((tiles,)),
            pltpu.SemaphoreType.DMA((tiles,)),
        ],
        compiler_params=pltpu.CompilerParams(
            collective_id=0,
            has_side_effects=True,
            dimension_semantics=("arbitrary", "arbitrary"),
            vmem_limit_bytes=60 * 1024 * 1024,
        ),
        name="bloch",
    )(wq, wk, moved)
    return result[..., :pairs]


def sums_kernel(electron_ref, phonon_ref, electron_out, phonon_out, got_e, got_p, send, recv_e, recv_p):
    bands, kas = lax.axis_size("pb"), lax.axis_size("ka")
    my_pb, my_ka = lax.axis_index("pb"), lax.axis_index("ka")
    barrier = pltpu.get_barrier_semaphore()
    for step in range(1, bands):
        pl.semaphore_signal(
            barrier, inc=1, device_id={"pb": lax.rem(my_pb + step, bands), "ka": my_ka},
            device_id_type=MESH,
        )
    for step in range(1, kas):
        pl.semaphore_signal(
            barrier, inc=1, device_id={"pb": my_pb, "ka": lax.rem(my_ka + step, kas)},
            device_id_type=MESH,
        )
    pl.semaphore_wait(barrier, bands + kas - 2)
    copies = []
    for step in range(1, bands):
        copies.append(pltpu.make_async_remote_copy(
            electron_ref, got_e.at[my_pb], send.at[step - 1], recv_e.at[step - 1],
            device_id={"pb": lax.rem(my_pb + step, bands), "ka": my_ka}, device_id_type=MESH,
        ))
    for step in range(1, kas):
        copies.append(pltpu.make_async_remote_copy(
            phonon_ref, got_p.at[my_ka], send.at[bands + step - 2], recv_p.at[step - 1],
            device_id={"pb": my_pb, "ka": lax.rem(my_ka + step, kas)}, device_id_type=MESH,
        ))
    for copy in copies:
        copy.start()
    got_e[my_pb] = electron_ref[...]
    got_p[my_ka] = phonon_ref[...]
    for copy in copies:
        copy.wait()
    total = got_e[0]
    for step in range(1, bands):
        total = total + got_e[step]
    electron_out[...] = total
    total = got_p[0]
    for step in range(1, kas):
        total = total + got_p[step]
    phonon_out[...] = total


def exchange(electron, phonon):
    bands, kas = lax.axis_size("pb"), lax.axis_size("ka")
    whole = pl.BlockSpec(memory_space=pltpu.VMEM)
    return pl.pallas_call(
        sums_kernel,
        in_specs=[whole, whole],
        out_specs=[whole, whole],
        out_shape=[
            jax.ShapeDtypeStruct(electron.shape, electron.dtype),
            jax.ShapeDtypeStruct(phonon.shape, phonon.dtype),
        ],
        scratch_shapes=[
            pltpu.VMEM((bands, *electron.shape), jnp.float32),
            pltpu.VMEM((kas, *phonon.shape), jnp.float32),
            pltpu.SemaphoreType.DMA((bands + kas - 2,)),
            pltpu.SemaphoreType.DMA((bands - 1,)),
            pltpu.SemaphoreType.DMA((kas - 1,)),
        ],
        compiler_params=pltpu.CompilerParams(collective_id=1, has_side_effects=True),
        name="sums",
    )(electron, phonon)


def angles(points, cells):
    product = lax.dot_general(
        points.astype(jnp.float32).astype(jnp.bfloat16),
        cells.astype(jnp.float32).astype(jnp.bfloat16),
        (((0,), (0,)), ((), ())),
        preferred_element_type=jnp.float32,
    )
    turns = jnp.floor((product + 0.5) * (1.0 / NG))
    angle = (product - turns * NG) * (2.0 * math.pi / NG)
    return jnp.cos(angle), jnp.sin(angle)


def whole_kernel(
    cells_block, tile, last, kpoints, qpoints, electron_cells, phonon_cells, modes, vectors,
    levels, filled, energy_k, occupation_k, omega, bose, x_ref, out_ref,
    wq, wk, half, parts, recv, rows_ref, emission, absorption, totals, got_e, got_p,
    send_sem, recv_sem, send_e, recv_e, send_p, recv_p,
):
    pairs_step = pl.program_id(0)
    cell_step = pl.program_id(1)
    tiles = pl.num_programs(0)
    cell_steps = pl.num_programs(1)
    bands, kas = lax.axis_size("pb"), lax.axis_size("ka")
    devices = bands * kas
    my_pb, my_ka = lax.axis_index("pb"), lax.axis_index("ka")
    me = my_pb * kas + my_ka
    columns = wq.shape[0]
    q_total = columns // 2
    cells = half.shape[1] // columns
    groups = parts.shape[2]
    mine = groups // bands
    rows = parts.shape[3] // 2
    q_local, k_local = vectors.shape[0], vectors.shape[1]
    barrier = pltpu.get_barrier_semaphore()

    @pl.when((pairs_step == 0) & (cell_step == 0))
    def _():
        def greet(step, carry):
            peer = lax.rem(me + step, devices)
            pl.semaphore_signal(
                barrier, inc=1, device_id={"pb": peer // kas, "ka": lax.rem(peer, kas)},
                device_id_type=MESH,
            )
            return carry

        lax.fori_loop(1, devices, greet, 0)
        cos, sin = angles(qpoints[...], phonon_cells[...])
        wq[...] = jnp.concatenate(
            [jnp.concatenate([cos, -sin], 1), jnp.concatenate([sin, cos], 1)], 0
        ).astype(jnp.bfloat16)
        table = electron_cells[...]
        own = table[:, :cells]
        for ka in range(1, kas):
            own = jnp.where(my_ka == ka, table[:, ka * cells : (ka + 1) * cells], own)
        cos, sin = angles(kpoints[...], own)
        blocks = []
        for ka in range(kas):
            c = cos[ka * k_local : (ka + 1) * k_local]
            s = sin[ka * k_local : (ka + 1) * k_local]
            blocks += [jnp.concatenate([c, -s], 1), jnp.concatenate([s, c], 1)]
        wk[...] = jnp.concatenate(blocks, 0).astype(jnp.bfloat16)

    @pl.when((pairs_step == 0) & (cell_step == 1))
    def _():
        for q in range(q_local):
            freq = omega[q : q + 1, :]
            boson = bose[q : q + 1, :]
            level_q = jnp.transpose(levels[q])
            filled_q = jnp.transpose(filled[q])
            for k in range(k_local):
                f = filled_q[:, k : k + 1]
                offset = energy_k[k] - level_q[:, k : k + 1]
                absorb = gaussian(offset + freq)
                emit = gaussian(offset - freq)
                emission[q, k] = (boson + f) * absorb + (boson + 1.0 - f) * emit
                absorption[q, k] = (occupation_k[k] - f) * absorb

    for cell in range(cells_block):
        right = jnp.concatenate([x_ref[0, cell], x_ref[1, cell]], axis=0)
        product = jnp.dot(wq[...], right, preferred_element_type=jnp.float32)
        row = cell_step * cells_block + cell
        for lane in range(tile // LANES):
            half[lane, pl.ds(row, columns, stride=cells), :] = product[
                :, lane * LANES : (lane + 1) * LANES
            ]

    def strip(index):
        start = pl.multiple_of(index * cells, cells)
        return jnp.concatenate(
            [half[lane, pl.ds(start, cells), :] for lane in range(tile // LANES)], axis=1
        ).astype(jnp.bfloat16)

    @pl.when(cell_step == cell_steps - 1)
    def _():
        def contract(group, carry):
            sums = []
            for member in range(2):
                q = group * 2 + member
                right = jnp.concatenate([strip(q), strip(q_total + q)], axis=0)
                sums.append(jnp.dot(wk[...], right, preferred_element_type=jnp.float32))
            for ka in range(kas):
                block = slice(ka * rows, (ka + 1) * rows)
                parts[pairs_step, ka, group] = jnp.concatenate(
                    [sums[0][block], sums[1][block]], axis=0
                ).astype(jnp.bfloat16)
            return carry

        lax.fori_loop(0, groups, contract, 0, unroll=4)

    @pl.when((cell_step == cell_steps - 1) & (pairs_step == 0))
    def _():
        pl.semaphore_wait(barrier, devices - 1)

    def send(index, width):
        def one(step, carry):
            peer = lax.rem(me + step, devices)
            to_pb, to_ka = peer // kas, lax.rem(peer, kas)
            pltpu.make_async_remote_copy(
                src_ref=parts.at[index, to_ka, pl.ds(to_pb * mine, mine), :, pl.ds(0, width)],
                dst_ref=recv.at[index, me, :, :, pl.ds(0, width)],
                send_sem=send_sem.at[index],
                recv_sem=recv_sem.at[index],
                device_id={"pb": to_pb, "ka": to_ka},
                device_id_type=MESH,
            ).start()
            return carry

        lax.fori_loop(1, devices, one, 0)

    @pl.when((cell_step == cell_steps - 1) & (pairs_step < tiles - 1))
    def _():
        send(pairs_step, tile)

    @pl.when((cell_step == cell_steps - 1) & (pairs_step == tiles - 1))
    def _():
        count = recv.shape[0]
        send(count - 1, last)
        for index in range(count):
            recv[index, me] = parts[index, my_ka, pl.ds(my_pb * mine, mine)]
        bands_n = rows_ref.shape[0] // (mine * 2 * rows)
        bands_own = bands_n // bands

        def piece(band, group, start):
            stop = start + MODES
            first, final = start // tile, (stop - 1) // tile
            out = []
            for index in range(first, final + 1):
                low, high = max(start, index * tile), min(stop, (index + 1) * tile)
                aligned = (low - index * tile) // LANES * LANES
                upper = -(-(high - index * tile) // LANES) * LANES
                total = recv[index, band * kas, group, :, aligned:upper].astype(jnp.float32)
                for ka in range(1, kas):
                    total = total + recv[
                        index, band * kas + ka, group, :, aligned:upper
                    ].astype(jnp.float32)
                out.append(
                    total[:, low - index * tile - aligned : high - index * tile - aligned]
                )
            return out[0] if len(out) == 1 else jnp.concatenate(out, axis=1)

        for index in range(count):
            width = tile if index < count - 1 else last
            window = recv.at[index, pl.ds(1, devices - 1), :, :, pl.ds(0, width)]
            pltpu.make_async_copy(window, window, recv_sem.at[index]).wait()
            for n in range(bands_own):
                if (n * MODES + MODES - 1) // tile != index:
                    continue
                for band in range(bands):
                    for group in range(mine):
                        row = group * 2 * rows * bands_n + band * bands_own + n
                        rows_ref[pl.ds(row, 2 * rows, stride=bands_n), :MODES] = piece(
                            band, group, n * MODES
                        )
        per_q = rows * bands_n
        side = per_q // 2
        electron = [None] * k_local
        for q in range(q_local):
            left = rows_ref[q * per_q : (q + 1) * per_q, :MODES].astype(jnp.bfloat16)
            by_real = jnp.dot(left, modes[q, 0], preferred_element_type=jnp.float32)
            by_imag = jnp.dot(left, modes[q, 1], preferred_element_type=jnp.float32)
            moded_real = by_real[:side] - by_imag[side:]
            moded_imag = by_imag[:side] + by_real[side:]
            phonon = None
            for k in range(k_local):
                u = jnp.concatenate(
                    [vectors[q, k, 0].astype(jnp.float32), vectors[q, k, 1].astype(jnp.float32)], 0
                ).astype(jnp.bfloat16)
                real = moded_real[k * bands_n : (k + 1) * bands_n]
                imag = moded_imag[k * bands_n : (k + 1) * bands_n]
                over = (((0,), (0,)), ((), ()))
                band_real = lax.dot_general(
                    u, jnp.concatenate([real, imag], 0).astype(jnp.bfloat16), over,
                    preferred_element_type=jnp.float32,
                )
                band_imag = lax.dot_general(
                    u, jnp.concatenate([imag, -real], 0).astype(jnp.bfloat16), over,
                    preferred_element_type=jnp.float32,
                )
                weight = band_real * band_real + band_imag * band_imag
                e_term = weight * emission[q, k]
                p_term = weight * absorption[q, k]
                electron[k] = e_term if q == 0 else electron[k] + e_term
                phonon = p_term if k == 0 else phonon + p_term
            totals[1, q : q + 1, :] = jnp.sum(phonon, axis=0, keepdims=True)
        for k in range(k_local):
            totals[0, k : k + 1, :] = jnp.sum(electron[k], axis=0, keepdims=True)
        copies = []
        for step in range(1, bands):
            copies.append(pltpu.make_async_remote_copy(
                totals.at[0], got_e.at[my_pb], send_e.at[step - 1], recv_e.at[step - 1],
                device_id={"pb": lax.rem(my_pb + step, bands), "ka": my_ka}, device_id_type=MESH,
            ))
        for step in range(1, kas):
            copies.append(pltpu.make_async_remote_copy(
                totals.at[1], got_p.at[my_ka], send_p.at[step - 1], recv_p.at[step - 1],
                device_id={"pb": my_pb, "ka": lax.rem(my_ka + step, kas)}, device_id_type=MESH,
            ))
        for copy in copies:
            copy.start()
        got_e[my_pb] = totals[0]
        got_p[my_ka] = totals[1]
        for index in range(count):
            width = tile if index < count - 1 else last
            window = recv.at[index, pl.ds(1, devices - 1), :, :, pl.ds(0, width)]
            pltpu.make_async_copy(window, window, send_sem.at[index]).wait()
        for copy in copies:
            copy.wait()
        total = got_e[0]
        for step in range(1, bands):
            total = total + got_e[step]
        out_ref[0] = total
        total = got_p[0]
        for step in range(1, kas):
            total = total + got_p[step]
        out_ref[1] = total


def everything(
    coupling, kpoints, qpoints, electron_cells, phonon_cells, phonon_modes, band_vectors,
    energies_kq, occupations_kq, energy_k, occupation_k, frequencies, bose_factors,
):
    bands, kas = lax.axis_size("pb"), lax.axis_size("ka")
    devices = bands * kas
    parts_count, cells, pairs, phonons = coupling.shape
    moved = jnp.transpose(coupling, (0, 1, 3, 2))
    padded = -(-pairs // LANES) * LANES
    tile = min(2 * LANES, padded)
    tiles = -(-padded // tile)
    last = padded - (tiles - 1) * tile
    cells_block = 16
    q_local, k_local = band_vectors.shape[0], band_vectors.shape[1]
    bands_n = band_vectors.shape[3]
    columns = 2 * qpoints.shape[1]
    groups = columns // 4
    mine = q_local // 2
    rows = 2 * k_local
    small = pl.BlockSpec(memory_space=pltpu.VMEM)
    scalars = pl.BlockSpec(memory_space=pltpu.SMEM)
    dma = pltpu.SemaphoreType.DMA
    result = pl.pallas_call(
        functools.partial(whole_kernel, cells_block, tile, last),
        grid=(tiles, cells // cells_block),
        in_specs=[small] * 8
        + [scalars] * 2
        + [small] * 2
        + [pl.BlockSpec((parts_count, cells_block, phonons, tile), lambda t, e: (0, e, 0, t))],
        out_specs=small,
        out_shape=jax.ShapeDtypeStruct((2, k_local, MODES), jnp.float32),
        scratch_shapes=[
            pltpu.VMEM((columns, 2 * phonons), jnp.bfloat16),
            pltpu.VMEM((2 * k_local * kas, 2 * cells), jnp.bfloat16),
            pltpu.VMEM((tile // LANES, columns * cells, LANES), jnp.float32),
            pltpu.VMEM((tiles, kas, groups, 2 * rows, tile), jnp.bfloat16),
            pltpu.VMEM((tiles, devices, mine, 2 * rows, tile), jnp.bfloat16),
            pltpu.VMEM((q_local * rows * bands_n, LANES), jnp.float32),
            pltpu.VMEM((q_local, k_local, bands_n, MODES), jnp.float32),
            pltpu.VMEM((q_local, k_local, bands_n, MODES), jnp.float32),
            pltpu.VMEM((2, k_local, MODES), jnp.float32),
            pltpu.VMEM((bands, k_local, MODES), jnp.float32),
            pltpu.VMEM((kas, k_local, MODES), jnp.float32),
            dma((tiles,)),
            dma((tiles,)),
            dma((bands - 1,)),
            dma((bands - 1,)),
            dma((kas - 1,)),
            dma((kas - 1,)),
        ],
        compiler_params=pltpu.CompilerParams(
            collective_id=2,
            has_side_effects=True,
            dimension_semantics=("arbitrary", "arbitrary"),
            vmem_limit_bytes=60 * 1024 * 1024,
        ),
        name="widths",
    )(
        kpoints, qpoints, electron_cells, phonon_cells, phonon_modes, band_vectors, energies_kq,
        occupations_kq, energy_k, occupation_k, frequencies, bose_factors, moved,
    )
    return result


def on_device(
    coupling,
    kpoints,
    qpoints,
    electron_cells,
    phonon_cells,
    phonon_modes,
    band_vectors,
    energies_kq,
    occupations_kq,
    energy_k,
    occupation_k,
    frequencies,
    bose_factors,
):
    k_local = energy_k.shape[0]
    q_local = frequencies.shape[0]
    cells_local = coupling.shape[1]
    bands, kas = lax.axis_size("pb"), lax.axis_size("ka")
    q_total = q_local * bands
    k_total = k_local * kas
    if coupling.shape[2] % MODES == 0 and k_local == q_local:
        sums = everything(
            coupling, kpoints, qpoints, electron_cells, phonon_cells, phonon_modes, band_vectors,
            energies_kq, occupations_kq, energy_k, occupation_k, frequencies, bose_factors,
        )
        return (sums[0] / (q_total * NB), sums[1] / (k_total * NB))
    cos_q, sin_q = phase_table(qpoints, phonon_cells)
    own_cells = lax.dynamic_slice_in_dim(
        electron_cells, lax.axis_index("ka") * cells_local, cells_local, 1
    )
    cos_k, sin_k = phase_table(kpoints, own_cells)
    wq = jnp.concatenate(
        [jnp.concatenate([cos_q, -sin_q], 1), jnp.concatenate([sin_q, cos_q], 1)], 0
    )
    wk = jnp.stack(
        [jnp.concatenate([cos_k, -sin_k], 1), jnp.concatenate([sin_k, cos_k], 1)], 1
    ).reshape(2 * k_total, 2 * cells_local)
    values = bloch(coupling, wq, wk, q_local, k_local)
    values = values.reshape(bands, q_local // 2, 2, k_local, 2, -1)
    values = jnp.transpose(values, (4, 3, 1, 2, 0, 5)).reshape(2, k_local, q_local, NB, MODES)
    electron, phonon = widths(
        values[0],
        values[1],
        phonon_modes,
        band_vectors,
        energies_kq,
        occupations_kq,
        energy_k,
        occupation_k,
        frequencies,
        bose_factors,
    )
    electron_width, phonon_width = exchange(electron / (q_total * NB), phonon / (k_total * NB))
    return (electron_width, phonon_width)


def solution(mesh):
    in_specs = (
        P(None, "ka", "pb", None),
        P(),
        P(),
        P(),
        P(),
        P("pb", None, None, None),
        P("pb", "ka", None, None, None),
        P("pb", "ka", None),
        P("pb", "ka", None),
        P("ka"),
        P("ka"),
        P("pb", None),
        P("pb", None),
    )
    out_specs = (P("ka", None), P("pb", None))
    return jax.shard_map(
        on_device, mesh=mesh, in_specs=in_specs, out_specs=out_specs, check_vma=False
    )
```

```python
import functools
import math

import jax
import jax.numpy as jnp
from jax import lax
from jax.experimental import pallas as pl
from jax.experimental.pallas import tpu as pltpu
from jax.sharding import PartitionSpec as P

NB = 40
MODES = 120
NG = 100


smearing = 0.05


def phase_table(points, cells):
    product = (
        points[0][:, None] * cells[0][None, :]
        + points[1][:, None] * cells[1][None, :]
        + points[2][:, None] * cells[2][None, :]
    )
    angle = jnp.mod(product, NG).astype(jnp.float32) * (2.0 * math.pi / NG)
    return (jnp.cos(angle).astype(jnp.bfloat16), jnp.sin(angle).astype(jnp.bfloat16))


def gaussian(offset):
    return jnp.exp(-0.5 * (offset / smearing) ** 2) / (smearing * math.sqrt(2.0 * math.pi))


def contract_last(left, right):
    return lax.dot_general(
        left, right, (((1,), (1,)), ((), ())), preferred_element_type=jnp.float32
    )


def mixed(form, left, right):
    return jnp.einsum(form, left, right, preferred_element_type=jnp.float32)


def widths(
    bloch_real, bloch_imag, modes, vectors, levels, filled, energy_k, occupation_k, omega, bose
):
    mode_real = modes[:, 0]
    mode_imag = modes[:, 1]
    moded_real = (
        mixed("kqnm,qmv->kqnv", bloch_real, mode_real)
        - mixed("kqnm,qmv->kqnv", bloch_imag, mode_imag)
    ).astype(jnp.bfloat16)
    moded_imag = (
        mixed("kqnm,qmv->kqnv", bloch_real, mode_imag)
        + mixed("kqnm,qmv->kqnv", bloch_imag, mode_real)
    ).astype(jnp.bfloat16)
    vector_real = vectors[:, :, 0]
    vector_imag = vectors[:, :, 1]
    band_real = mixed("qknb,kqnv->kqbv", vector_real, moded_real) + mixed(
        "qknb,kqnv->kqbv", vector_imag, moded_imag
    )
    band_imag = mixed("qknb,kqnv->kqbv", vector_real, moded_imag) - mixed(
        "qknb,kqnv->kqbv", vector_imag, moded_real
    )
    weight = band_real * band_real + band_imag * band_imag
    level_kq = jnp.transpose(levels, (1, 0, 2))[..., None]
    filled_kq = jnp.transpose(filled, (1, 0, 2))[..., None]
    offset = energy_k[:, None, None, None] - level_kq
    freq = omega[None, :, None, :]
    boson = bose[None, :, None, :]
    absorb = gaussian(offset + freq)
    emit = gaussian(offset - freq)
    electron = jnp.sum(
        weight * ((boson + filled_kq) * absorb + (boson + 1.0 - filled_kq) * emit), axis=(1, 2)
    )
    phonon = jnp.sum(weight * (occupation_k[:, None, None, None] - filled_kq) * absorb, axis=(0, 2))
    return (electron, phonon)


MESH = pl.DeviceIdType.MESH
LANES = 128


def bloch_kernel(
    cells_block, tile, last, wq_ref, wk_ref, x_ref, out_ref,
    half, parts, recv, send_sem, recv_sem,
):
    pairs_step = pl.program_id(0)
    cell_step = pl.program_id(1)
    tiles = pl.num_programs(0)
    cell_steps = pl.num_programs(1)
    bands, kas = lax.axis_size("pb"), lax.axis_size("ka")
    devices = bands * kas
    me = lax.axis_index("pb") * kas + lax.axis_index("ka")
    columns = wq_ref.shape[0]
    cells = half.shape[1] // columns
    groups = parts.shape[2]
    mine = groups // bands
    rows = parts.shape[3] // 2
    barrier = pltpu.get_barrier_semaphore()

    @pl.when((pairs_step == 0) & (cell_step == 0))
    def _():
        def greet(step, carry):
            peer = lax.rem(me + step, devices)
            pl.semaphore_signal(
                barrier, inc=1, device_id={"pb": peer // kas, "ka": lax.rem(peer, kas)},
                device_id_type=MESH,
            )
            return carry

        lax.fori_loop(1, devices, greet, 0)

    for cell in range(cells_block):
        right = jnp.concatenate([x_ref[0, cell], x_ref[1, cell]], axis=0)
        product = jnp.dot(wq_ref[...], right, preferred_element_type=jnp.float32)
        row = cell_step * cells_block + cell
        for lane in range(tile // LANES):
            half[lane, pl.ds(row, columns, stride=cells), :] = product[
                :, lane * LANES : (lane + 1) * LANES
            ]

    def strip(index):
        start = pl.multiple_of(index * cells, cells)
        return jnp.concatenate(
            [half[lane, pl.ds(start, cells), :] for lane in range(tile // LANES)], axis=1
        ).astype(jnp.bfloat16)

    @pl.when(cell_step == cell_steps - 1)
    def _():
        def contract(group, carry):
            sums = []
            for member in range(2):
                q = group * 2 + member
                right = jnp.concatenate([strip(q), strip(columns // 2 + q)], axis=0)
                sums.append(
                    jnp.dot(wk_ref[...], right, preferred_element_type=jnp.float32)
                )
            for ka in range(kas):
                block = slice(ka * rows, (ka + 1) * rows)
                parts[pairs_step, ka, group] = jnp.concatenate(
                    [sums[0][block], sums[1][block]], axis=0
                ).astype(jnp.bfloat16)
            return carry

        lax.fori_loop(0, groups, contract, 0, unroll=4)

    @pl.when((cell_step == cell_steps - 1) & (pairs_step == 0))
    def _():
        pl.semaphore_wait(barrier, devices - 1)

    def send(index, width):
        def one(step, carry):
            peer = lax.rem(me + step, devices)
            to_pb, to_ka = peer // kas, lax.rem(peer, kas)
            pltpu.make_async_remote_copy(
                src_ref=parts.at[index, to_ka, pl.ds(to_pb * mine, mine), :, pl.ds(0, width)],
                dst_ref=recv.at[index, me, :, :, pl.ds(0, width)],
                send_sem=send_sem.at[index],
                recv_sem=recv_sem.at[index],
                device_id={"pb": to_pb, "ka": to_ka},
                device_id_type=MESH,
            ).start()
            return carry

        lax.fori_loop(1, devices, one, 0)

    @pl.when((cell_step == cell_steps - 1) & (pairs_step < tiles - 1))
    def _():
        send(pairs_step, tile)

    @pl.when((cell_step == cell_steps - 1) & (pairs_step == tiles - 1))
    def _():
        count = recv.shape[0]
        send(count - 1, last)
        my_pb, my_ka = lax.axis_index("pb"), lax.axis_index("ka")
        for index in range(count):
            recv[index, me] = parts[index, my_ka, pl.ds(my_pb * mine, mine)]
        for index in range(count):
            width = tile if index < count - 1 else last
            window = recv.at[index, pl.ds(1, devices - 1), :, :, pl.ds(0, width)]
            pltpu.make_async_copy(window, window, send_sem.at[index]).wait()
            pltpu.make_async_copy(window, window, recv_sem.at[index]).wait()
            for band in range(bands):
                total = recv[index, band * kas, :, :, :width].astype(jnp.float32)
                for ka in range(1, kas):
                    total = total + recv[index, band * kas + ka, :, :, :width].astype(jnp.float32)
                out_ref[band, :, :, index * tile : index * tile + width] = total.astype(
                    jnp.bfloat16
                )


def bloch(coupling, wq, wk, q_local, k_local):
    bands, kas = lax.axis_size("pb"), lax.axis_size("ka")
    devices = bands * kas
    parts_count, cells, pairs, phonons = coupling.shape
    moved = jnp.transpose(coupling, (0, 1, 3, 2))
    padded = -(-pairs // LANES) * LANES
    if pairs < LANES:
        moved = jnp.pad(moved, ((0, 0), (0, 0), (0, 0), (0, LANES - pairs)))
    tile = min(2 * LANES, padded)
    tiles = -(-padded // tile)
    last = padded - (tiles - 1) * tile
    cells_block = 16
    columns = wq.shape[0]
    groups = columns // 4
    mine = q_local // 2
    rows = 4 * k_local
    result = pl.pallas_call(
        functools.partial(bloch_kernel, cells_block, tile, last),
        grid=(tiles, cells // cells_block),
        in_specs=[
            pl.BlockSpec(wq.shape, lambda t, e: (0, 0)),
            pl.BlockSpec(wk.shape, lambda t, e: (0, 0)),
            pl.BlockSpec((parts_count, cells_block, phonons, tile), lambda t, e: (0, e, 0, t)),
        ],
        out_specs=pl.BlockSpec((bands, mine, rows, padded), lambda t, e: (0, 0, 0, 0)),
        out_shape=jax.ShapeDtypeStruct((bands, mine, rows, padded), jnp.bfloat16),
        scratch_shapes=[
            pltpu.VMEM((tile // LANES, columns * cells, LANES), jnp.float32),
            pltpu.VMEM((tiles, kas, groups, rows, tile), jnp.bfloat16),
            pltpu.VMEM((tiles, devices, mine, rows, tile), jnp.bfloat16),
            pltpu.SemaphoreType.DMA((tiles,)),
            pltpu.SemaphoreType.DMA((tiles,)),
        ],
        compiler_params=pltpu.CompilerParams(
            collective_id=0,
            has_side_effects=True,
            dimension_semantics=("arbitrary", "arbitrary"),
            vmem_limit_bytes=60 * 1024 * 1024,
        ),
        name="bloch",
    )(wq, wk, moved)
    return result[..., :pairs]


def sums_kernel(electron_ref, phonon_ref, electron_out, phonon_out, got_e, got_p, send, recv_e, recv_p):
    bands, kas = lax.axis_size("pb"), lax.axis_size("ka")
    my_pb, my_ka = lax.axis_index("pb"), lax.axis_index("ka")
    barrier = pltpu.get_barrier_semaphore()
    for step in range(1, bands):
        pl.semaphore_signal(
            barrier, inc=1, device_id={"pb": lax.rem(my_pb + step, bands), "ka": my_ka},
            device_id_type=MESH,
        )
    for step in range(1, kas):
        pl.semaphore_signal(
            barrier, inc=1, device_id={"pb": my_pb, "ka": lax.rem(my_ka + step, kas)},
            device_id_type=MESH,
        )
    pl.semaphore_wait(barrier, bands + kas - 2)
    copies = []
    for step in range(1, bands):
        copies.append(pltpu.make_async_remote_copy(
            electron_ref, got_e.at[my_pb], send.at[step - 1], recv_e.at[step - 1],
            device_id={"pb": lax.rem(my_pb + step, bands), "ka": my_ka}, device_id_type=MESH,
        ))
    for step in range(1, kas):
        copies.append(pltpu.make_async_remote_copy(
            phonon_ref, got_p.at[my_ka], send.at[bands + step - 2], recv_p.at[step - 1],
            device_id={"pb": my_pb, "ka": lax.rem(my_ka + step, kas)}, device_id_type=MESH,
        ))
    for copy in copies:
        copy.start()
    got_e[my_pb] = electron_ref[...]
    got_p[my_ka] = phonon_ref[...]
    for copy in copies:
        copy.wait()
    total = got_e[0]
    for step in range(1, bands):
        total = total + got_e[step]
    electron_out[...] = total
    total = got_p[0]
    for step in range(1, kas):
        total = total + got_p[step]
    phonon_out[...] = total


def exchange(electron, phonon):
    bands, kas = lax.axis_size("pb"), lax.axis_size("ka")
    whole = pl.BlockSpec(memory_space=pltpu.VMEM)
    return pl.pallas_call(
        sums_kernel,
        in_specs=[whole, whole],
        out_specs=[whole, whole],
        out_shape=[
            jax.ShapeDtypeStruct(electron.shape, electron.dtype),
            jax.ShapeDtypeStruct(phonon.shape, phonon.dtype),
        ],
        scratch_shapes=[
            pltpu.VMEM((bands, *electron.shape), jnp.float32),
            pltpu.VMEM((kas, *phonon.shape), jnp.float32),
            pltpu.SemaphoreType.DMA((bands + kas - 2,)),
            pltpu.SemaphoreType.DMA((bands - 1,)),
            pltpu.SemaphoreType.DMA((kas - 1,)),
        ],
        compiler_params=pltpu.CompilerParams(collective_id=1, has_side_effects=True),
        name="sums",
    )(electron, phonon)


def angles(points, cells):
    product = lax.dot_general(
        points.astype(jnp.float32).astype(jnp.bfloat16),
        cells.astype(jnp.float32).astype(jnp.bfloat16),
        (((0,), (0,)), ((), ())),
        preferred_element_type=jnp.float32,
    )
    turns = jnp.floor((product + 0.5) * (1.0 / NG))
    angle = (product - turns * NG) * (2.0 * math.pi / NG)
    return jnp.cos(angle), jnp.sin(angle)


def whole_kernel(
    cells_block, tile, last, kpoints, qpoints, electron_cells, phonon_cells, modes, vectors,
    levels, filled, energy_k, occupation_k, omega, bose, x_ref, out_ref,
    wq, wk, half, parts, recv, rows_ref, emission, absorption, totals, got_e, got_p,
    send_sem, recv_sem, send_e, recv_e, send_p, recv_p,
):
    pairs_step = pl.program_id(0)
    cell_step = pl.program_id(1)
    tiles = pl.num_programs(0)
    cell_steps = pl.num_programs(1)
    bands, kas = lax.axis_size("pb"), lax.axis_size("ka")
    devices = bands * kas
    my_pb, my_ka = lax.axis_index("pb"), lax.axis_index("ka")
    me = my_pb * kas + my_ka
    columns = wq.shape[0]
    q_total = columns // 2
    cells = half.shape[1] // columns
    groups = parts.shape[2]
    mine = groups // bands
    rows = parts.shape[3] // 2
    q_local, k_local = vectors.shape[0], vectors.shape[1]
    barrier = pltpu.get_barrier_semaphore()

    @pl.when((pairs_step == 0) & (cell_step == 0))
    def _():
        def greet(step, carry):
            peer = lax.rem(me + step, devices)
            pl.semaphore_signal(
                barrier, inc=1, device_id={"pb": peer // kas, "ka": lax.rem(peer, kas)},
                device_id_type=MESH,
            )
            return carry

        lax.fori_loop(1, devices, greet, 0)
        cos, sin = angles(qpoints[...], phonon_cells[...])
        wq[...] = jnp.concatenate(
            [jnp.concatenate([cos, -sin], 1), jnp.concatenate([sin, cos], 1)], 0
        ).astype(jnp.bfloat16)
        table = electron_cells[...]
        own = table[:, :cells]
        for ka in range(1, kas):
            own = jnp.where(my_ka == ka, table[:, ka * cells : (ka + 1) * cells], own)
        cos, sin = angles(kpoints[...], own)
        blocks = []
        for ka in range(kas):
            c = cos[ka * k_local : (ka + 1) * k_local]
            s = sin[ka * k_local : (ka + 1) * k_local]
            blocks += [jnp.concatenate([c, -s], 1), jnp.concatenate([s, c], 1)]
        wk[...] = jnp.concatenate(blocks, 0).astype(jnp.bfloat16)

    @pl.when((pairs_step == jnp.minimum(tiles - 1, 1)) & (cell_step == 0))
    def _():
        for q in range(q_local):
            freq = omega[q : q + 1, :]
            boson = bose[q : q + 1, :]
            level_q = jnp.transpose(levels[q])
            filled_q = jnp.transpose(filled[q])
            for k in range(k_local):
                f = filled_q[:, k : k + 1]
                offset = energy_k[k] - level_q[:, k : k + 1]
                absorb = gaussian(offset + freq)
                emit = gaussian(offset - freq)
                emission[q, k] = (boson + f) * absorb + (boson + 1.0 - f) * emit
                absorption[q, k] = (occupation_k[k] - f) * absorb

    def project(chunk, carry):
        for step in range(cells_block // 2):
            cell = chunk * (cells_block // 2) + step
            right = jnp.concatenate([x_ref[0, cell], x_ref[1, cell]], axis=0)
            product = jnp.dot(wq[...], right, preferred_element_type=jnp.float32)
            row = cell_step * cells_block + cell
            for lane in range(tile // LANES):
                half[lane, pl.ds(row, columns, stride=cells), :] = product[
                    :, lane * LANES : (lane + 1) * LANES
                ]
        return carry

    lax.fori_loop(0, 2, project, 0)

    def strip(index):
        start = pl.multiple_of(index * cells, cells)
        return jnp.concatenate(
            [half[lane, pl.ds(start, cells), :] for lane in range(tile // LANES)], axis=1
        ).astype(jnp.bfloat16)

    @pl.when(cell_step == cell_steps - 1)
    def _():
        def contract(group, carry):
            sums = []
            for member in range(2):
                q = group * 2 + member
                right = jnp.concatenate([strip(q), strip(q_total + q)], axis=0)
                sums.append(jnp.dot(wk[...], right, preferred_element_type=jnp.float32))
            for ka in range(kas):
                block = slice(ka * rows, (ka + 1) * rows)
                parts[pairs_step, ka, group] = jnp.concatenate(
                    [sums[0][block], sums[1][block]], axis=0
                ).astype(jnp.bfloat16)
            return carry

        lax.fori_loop(0, groups, contract, 0, unroll=4)

    @pl.when((cell_step == cell_steps - 1) & (pairs_step == 0))
    def _():
        pl.semaphore_wait(barrier, devices - 1)

    def send(index, width):
        def one(step, carry):
            peer = lax.rem(me + step, devices)
            to_pb, to_ka = peer // kas, lax.rem(peer, kas)
            pltpu.make_async_remote_copy(
                src_ref=parts.at[index, to_ka, pl.ds(to_pb * mine, mine), :, pl.ds(0, width)],
                dst_ref=recv.at[index, me, :, :, pl.ds(0, width)],
                send_sem=send_sem.at[index],
                recv_sem=recv_sem.at[index],
                device_id={"pb": to_pb, "ka": to_ka},
                device_id_type=MESH,
            ).start()
            return carry

        lax.fori_loop(1, devices, one, 0)

    @pl.when((cell_step == cell_steps - 1) & (pairs_step < tiles - 1))
    def _():
        send(pairs_step, tile)

    @pl.when((cell_step == cell_steps - 1) & (pairs_step == tiles - 1))
    def _():
        count = recv.shape[0]
        send(count - 1, last)
        for index in range(count):
            recv[index, me] = parts[index, my_ka, pl.ds(my_pb * mine, mine)]
        bands_n = rows_ref.shape[0] // (mine * 2 * rows)
        bands_own = bands_n // bands

        def piece(band, group, start):
            stop = start + MODES
            first, final = start // tile, (stop - 1) // tile
            out = []
            for index in range(first, final + 1):
                low, high = max(start, index * tile), min(stop, (index + 1) * tile)
                aligned = (low - index * tile) // LANES * LANES
                upper = -(-(high - index * tile) // LANES) * LANES
                total = recv[index, band * kas, group, :, aligned:upper].astype(jnp.float32)
                for ka in range(1, kas):
                    total = total + recv[
                        index, band * kas + ka, group, :, aligned:upper
                    ].astype(jnp.float32)
                out.append(
                    total[:, low - index * tile - aligned : high - index * tile - aligned]
                )
            return out[0] if len(out) == 1 else jnp.concatenate(out, axis=1)

        for index in range(count):
            width = tile if index < count - 1 else last
            window = recv.at[index, pl.ds(1, devices - 1), :, :, pl.ds(0, width)]
            pltpu.make_async_copy(window, window, recv_sem.at[index]).wait()
            for n in range(bands_own):
                if (n * MODES + MODES - 1) // tile != index:
                    continue
                for band in range(bands):
                    for group in range(mine):
                        row = group * 2 * rows * bands_n + band * bands_own + n
                        rows_ref[pl.ds(row, 2 * rows, stride=bands_n), :MODES] = piece(
                            band, group, n * MODES
                        )
        per_q = rows * bands_n
        side = per_q // 2
        electron = [None] * k_local
        for q in range(q_local):
            left = rows_ref[q * per_q : (q + 1) * per_q, :MODES].astype(jnp.bfloat16)
            by_real = jnp.dot(left, modes[q, 0], preferred_element_type=jnp.float32)
            by_imag = jnp.dot(left, modes[q, 1], preferred_element_type=jnp.float32)
            moded_real = by_real[:side] - by_imag[side:]
            moded_imag = by_imag[:side] + by_real[side:]
            phonon = None
            for k in range(k_local):
                u = jnp.concatenate(
                    [vectors[q, k, 0].astype(jnp.float32), vectors[q, k, 1].astype(jnp.float32)], 0
                ).astype(jnp.bfloat16)
                real = moded_real[k * bands_n : (k + 1) * bands_n]
                imag = moded_imag[k * bands_n : (k + 1) * bands_n]
                over = (((0,), (0,)), ((), ()))
                band_real = lax.dot_general(
                    u, jnp.concatenate([real, imag], 0).astype(jnp.bfloat16), over,
                    preferred_element_type=jnp.float32,
                )
                band_imag = lax.dot_general(
                    u, jnp.concatenate([imag, -real], 0).astype(jnp.bfloat16), over,
                    preferred_element_type=jnp.float32,
                )
                weight = band_real * band_real + band_imag * band_imag
                e_term = weight * emission[q, k]
                p_term = weight * absorption[q, k]
                electron[k] = e_term if q == 0 else electron[k] + e_term
                phonon = p_term if k == 0 else phonon + p_term
            totals[1, q : q + 1, :] = jnp.sum(phonon, axis=0, keepdims=True)
        for k in range(k_local):
            totals[0, k : k + 1, :] = jnp.sum(electron[k], axis=0, keepdims=True)
        copies = []
        for step in range(1, bands):
            copies.append(pltpu.make_async_remote_copy(
                totals.at[0], got_e.at[my_pb], send_e.at[step - 1], recv_e.at[step - 1],
                device_id={"pb": lax.rem(my_pb + step, bands), "ka": my_ka}, device_id_type=MESH,
            ))
        for step in range(1, kas):
            copies.append(pltpu.make_async_remote_copy(
                totals.at[1], got_p.at[my_ka], send_p.at[step - 1], recv_p.at[step - 1],
                device_id={"pb": my_pb, "ka": lax.rem(my_ka + step, kas)}, device_id_type=MESH,
            ))
        for copy in copies:
            copy.start()
        got_e[my_pb] = totals[0]
        got_p[my_ka] = totals[1]
        for index in range(count):
            width = tile if index < count - 1 else last
            window = recv.at[index, pl.ds(1, devices - 1), :, :, pl.ds(0, width)]
            pltpu.make_async_copy(window, window, send_sem.at[index]).wait()
        for copy in copies:
            copy.wait()
        total = got_e[0]
        for step in range(1, bands):
            total = total + got_e[step]
        out_ref[0] = total
        total = got_p[0]
        for step in range(1, kas):
            total = total + got_p[step]
        out_ref[1] = total


def everything(
    coupling, kpoints, qpoints, electron_cells, phonon_cells, phonon_modes, band_vectors,
    energies_kq, occupations_kq, energy_k, occupation_k, frequencies, bose_factors,
):
    bands, kas = lax.axis_size("pb"), lax.axis_size("ka")
    devices = bands * kas
    parts_count, cells, pairs, phonons = coupling.shape
    moved = jnp.transpose(coupling, (0, 1, 3, 2))
    padded = -(-pairs // LANES) * LANES
    tile = LANES
    tiles = -(-padded // tile)
    last = padded - (tiles - 1) * tile
    cells_block = cells
    q_local, k_local = band_vectors.shape[0], band_vectors.shape[1]
    bands_n = band_vectors.shape[3]
    columns = 2 * qpoints.shape[1]
    groups = columns // 4
    mine = q_local // 2
    rows = 2 * k_local
    small = pl.BlockSpec(memory_space=pltpu.VMEM)
    scalars = pl.BlockSpec(memory_space=pltpu.SMEM)
    dma = pltpu.SemaphoreType.DMA
    result = pl.pallas_call(
        functools.partial(whole_kernel, cells_block, tile, last),
        grid=(tiles, cells // cells_block),
        in_specs=[small] * 8
        + [scalars] * 2
        + [small] * 2
        + [pl.BlockSpec((parts_count, cells_block, phonons, tile), lambda t, e: (0, e, 0, t))],
        out_specs=small,
        out_shape=jax.ShapeDtypeStruct((2, k_local, MODES), jnp.float32),
        scratch_shapes=[
            pltpu.VMEM((columns, 2 * phonons), jnp.bfloat16),
            pltpu.VMEM((2 * k_local * kas, 2 * cells), jnp.bfloat16),
            pltpu.VMEM((tile // LANES, columns * cells, LANES), jnp.float32),
            pltpu.VMEM((tiles, kas, groups, 2 * rows, tile), jnp.bfloat16),
            pltpu.VMEM((tiles, devices, mine, 2 * rows, tile), jnp.bfloat16),
            pltpu.VMEM((q_local * rows * bands_n, LANES), jnp.float32),
            pltpu.VMEM((q_local, k_local, bands_n, MODES), jnp.float32),
            pltpu.VMEM((q_local, k_local, bands_n, MODES), jnp.float32),
            pltpu.VMEM((2, k_local, MODES), jnp.float32),
            pltpu.VMEM((bands, k_local, MODES), jnp.float32),
            pltpu.VMEM((kas, k_local, MODES), jnp.float32),
            dma((tiles,)),
            dma((tiles,)),
            dma((bands - 1,)),
            dma((bands - 1,)),
            dma((kas - 1,)),
            dma((kas - 1,)),
        ],
        compiler_params=pltpu.CompilerParams(
            collective_id=2,
            has_side_effects=True,
            dimension_semantics=("arbitrary", "arbitrary"),
            vmem_limit_bytes=60 * 1024 * 1024,
        ),
        name="widths",
    )(
        kpoints, qpoints, electron_cells, phonon_cells, phonon_modes, band_vectors, energies_kq,
        occupations_kq, energy_k, occupation_k, frequencies, bose_factors, moved,
    )
    return result


def on_device(
    coupling,
    kpoints,
    qpoints,
    electron_cells,
    phonon_cells,
    phonon_modes,
    band_vectors,
    energies_kq,
    occupations_kq,
    energy_k,
    occupation_k,
    frequencies,
    bose_factors,
):
    k_local = energy_k.shape[0]
    q_local = frequencies.shape[0]
    cells_local = coupling.shape[1]
    bands, kas = lax.axis_size("pb"), lax.axis_size("ka")
    q_total = q_local * bands
    k_total = k_local * kas
    if coupling.shape[2] % MODES == 0 and k_local == q_local:
        sums = everything(
            coupling, kpoints, qpoints, electron_cells, phonon_cells, phonon_modes, band_vectors,
            energies_kq, occupations_kq, energy_k, occupation_k, frequencies, bose_factors,
        )
        return (sums[0] / (q_total * NB), sums[1] / (k_total * NB))
    cos_q, sin_q = phase_table(qpoints, phonon_cells)
    own_cells = lax.dynamic_slice_in_dim(
        electron_cells, lax.axis_index("ka") * cells_local, cells_local, 1
    )
    cos_k, sin_k = phase_table(kpoints, own_cells)
    wq = jnp.concatenate(
        [jnp.concatenate([cos_q, -sin_q], 1), jnp.concatenate([sin_q, cos_q], 1)], 0
    )
    wk = jnp.stack(
        [jnp.concatenate([cos_k, -sin_k], 1), jnp.concatenate([sin_k, cos_k], 1)], 1
    ).reshape(2 * k_total, 2 * cells_local)
    values = bloch(coupling, wq, wk, q_local, k_local)
    values = values.reshape(bands, q_local // 2, 2, k_local, 2, -1)
    values = jnp.transpose(values, (4, 3, 1, 2, 0, 5)).reshape(2, k_local, q_local, NB, MODES)
    electron, phonon = widths(
        values[0],
        values[1],
        phonon_modes,
        band_vectors,
        energies_kq,
        occupations_kq,
        energy_k,
        occupation_k,
        frequencies,
        bose_factors,
    )
    electron_width, phonon_width = exchange(electron / (q_total * NB), phonon / (k_total * NB))
    return (electron_width, phonon_width)


def solution(mesh):
    in_specs = (
        P(None, "ka", "pb", None),
        P(),
        P(),
        P(),
        P(),
        P("pb", None, None, None),
        P("pb", "ka", None, None, None),
        P("pb", "ka", None),
        P("pb", "ka", None),
        P("ka"),
        P("ka"),
        P("pb", None),
        P("pb", None),
    )
    out_specs = (P("ka", None), P("pb", None))
    return jax.shard_map(
        on_device, mesh=mesh, in_specs=in_specs, out_specs=out_specs, check_vma=False
    )
```
